32 devices in a mesh: dp: 2 (over x), feat: 16 (over z, y, core).
Axes of the slice: x: 2, y: 2, z: 4, core: 2. Of those that a mesh axis runs over, the one named last changes fastest.
Arguments:
- inputs: bfloat16 [1024, 8192], P('dp', 'feat'), may hold values from -6 to 6
- bfly: bfloat16 [64, 7, 128, 512], P('feat'), may hold values from -0.1875 to 0.1875
- lr_u: bfloat16 [8192, 256], P('feat'), may hold values from -0.0625 to 0.0625
- lr_v: bfloat16 [256, 32768], P(None, 'feat'), may hold values from -0.375 to 0.375
- cotangent: bfloat16 [1024, 32768], P('dp', 'feat'), may hold values from -6 to 6
Outputs:
- activated: bfloat16 [1024, 32768], P('dp', 'feat')
- d_inputs: bfloat16 [1024, 8192], P('dp', 'feat')
- d_bfly: float32 [64, 7, 128, 512], P('feat')
- d_u: float32 [8192, 256], P('feat')
- d_v: float32 [256, 32768], P(None, 'feat')
The draws below stay inside these ranges and needn't reach their ends.
All inputs are finite; a program needn't handle non-finite values.
Results may differ from the reference program's by a relative error of at most 0.0065.
Values may be sent and summed in bfloat16 or wider, within the bound.
No kernel may reach another device: no remote copies, remote signals or barrier semaphores. Data moves between devices by JAX's collectives and lax.ppermute only.
A program may use at most 128 MiB of HBM per device.

```python
import jax
import jax.numpy as jnp
from jax import lax

D = 8192
FF = 32768
R = 256
BLK = 128
LOG = 6
S = 7
NB = 64
FG = 512
TOKENS = 1024


def block_scale(rng, extent, pieces, smallest, high):
    loudness = 1.0
    for position, shards_of in pieces:
        steps = jax.random.uniform(jax.random.fold_in(jax.random.fold_in(rng, 6), position), (shards_of,), jnp.float32, smallest / len(pieces), high / len(pieces))
        loudness = loudness * jnp.repeat(jnp.exp(steps), extent[position] // shards_of).reshape((-1,) + (1,) * (len(extent) - 1 - position))
    return loudness


def gaussian(rng, extent, deviation, reach, shards=(), kind=jnp.bfloat16):
    entries = jax.random.normal(rng, extent, jnp.float32) * deviation
    if len(shards) > 0:
        entries = block_scale(rng, extent, shards, -0.22, 0.18) * entries
    return jnp.clip(entries, min=-reach, max=reach).astype(kind)


def setup_inputs(seed: int = 0) -> dict:
    arg_keys = jax.random.split(jax.random.key(seed), 6)
    return {
        "inputs": gaussian(arg_keys[0], (TOKENS, D), 1.0, 6.0, ((0, 2), (1, 16))),
        "bfly": gaussian(arg_keys[1], (NB, S, BLK, FG), (S * BLK) ** -0.5, 0.1875, ((0, 16),)),
        "lr_u": gaussian(arg_keys[2], (D, R), D ** -0.5, 0.0625, ((0, 16),)),
        "lr_v": gaussian(arg_keys[3], (R, FF), R ** -0.5, 0.375, ((1, 16),)),
        "cotangent": gaussian(arg_keys[4], (TOKENS, FF), 1.0, 6.0, ((0, 2), (1, 16))),
    }


def gelu_tanh(value):
    return jax.nn.gelu(value, approximate=True)

def reference(inputs, bfly, lr_u, lr_v, cotangent):
    tokens = inputs.shape[0]
    blocks = inputs.reshape(tokens, NB, BLK).astype(jnp.float32)
    weights = bfly.astype(jnp.float32)
    index = jnp.arange(NB, dtype=jnp.int32)
    butterfly = jnp.zeros((tokens, NB, FG), jnp.float32)
    orders = []
    for section in range(S):
        order = index ^ 1 << section if section < LOG else index
        orders.append(order)
        butterfly = butterfly + jnp.einsum('tbi,bio->tbo', blocks[:, order], weights[:, section])
    low = jnp.dot(inputs, lr_u, preferred_element_type=jnp.float32).astype(jnp.bfloat16)
    pre = butterfly.reshape(tokens, FF) + jnp.dot(low, lr_v, preferred_element_type=jnp.float32)
    activated, backward = jax.vjp(gelu_tanh, pre)
    d_pre = backward(cotangent.astype(jnp.float32))[0].astype(jnp.bfloat16)
    d_low = jnp.dot(d_pre, lr_v.T, preferred_element_type=jnp.float32).astype(jnp.bfloat16)
    grad_groups = d_pre.reshape(tokens, NB, FG).astype(jnp.float32)
    d_inputs = jnp.dot(d_low, lr_u.T, preferred_element_type=jnp.float32).reshape(tokens, NB, BLK)
    tiles = []
    for section in range(S):
        order = orders[section]
        term = lax.optimization_barrier(jnp.einsum('tbo,bio->tbi', grad_groups, weights[:, section]).astype(jnp.bfloat16)).astype(jnp.float32)
        d_inputs = d_inputs + term[:, order]
        tiles.append(jnp.einsum('tbi,tbo->bio', blocks[:, order], grad_groups))
    scale = 1.0 / jnp.sqrt(jnp.float32(TOKENS))
    d_bfly = jnp.stack(tiles, axis=1) * scale
    d_u = jnp.dot(inputs.T, d_low, preferred_element_type=jnp.float32) * scale
    d_v = jnp.dot(low.T, d_pre, preferred_element_type=jnp.float32) * scale
    return (activated.astype(jnp.bfloat16), d_inputs.reshape(tokens, D).astype(jnp.bfloat16), d_bfly, d_u, d_v)
```

```python
import functools

import jax
import jax.numpy as jnp
import numpy as np
from jax import lax
from jax.experimental import pallas as pl
from jax.experimental.pallas import tpu as pltpu
from jax.sharding import PartitionSpec as P

BF = jnp.bfloat16
F32 = jnp.float32
VMEM_LIMIT = 48 * 1024 * 1024
GELU_C = float(np.sqrt(2.0 / np.pi))
GELU_A = 0.044715


def crossed(block, axis, mask):
    count = lax.axis_size(axis)
    return lax.ppermute(block, axis, [(i, i ^ mask) for i in range(count)])


def rolled(block, axis, shift):
    count = lax.axis_size(axis)
    return lax.ppermute(block, axis, [(i, (i + shift) % count) for i in range(count)])


def scatter_half(part, bit, axis):
    rows = part.shape[0] // 2
    mine = (lax.axis_index(axis) >> bit) & 1
    keep = lax.dynamic_slice_in_dim(part, mine * rows, rows, 0)
    send = lax.dynamic_slice_in_dim(part, (1 - mine) * rows, rows, 0)
    return keep + crossed(send.astype(BF), axis, 1 << bit).astype(F32)


def gather_half(part, bit, axis):
    mine = (lax.axis_index(axis) >> bit) & 1
    other = crossed(part, axis, 1 << bit)
    low = jnp.where(mine == 0, part, other)
    high = jnp.where(mine == 0, other, part)
    return jnp.concatenate([low, high], 0)


def reduce_feat(part, axis):
    bits = lax.axis_size(axis).bit_length() - 1
    near = min(bits, 2)
    for bit in range(near):
        part = scatter_half(part, bit, axis)
    sent = part.astype(BF)
    for other in range(1, 1 << (bits - near)):
        part = part + crossed(sent, axis, other << near).astype(F32)
    part = part.astype(BF)
    for bit in range(near - 1, 0, -1):
        part = gather_half(part, bit, axis)
    return part


def finish_feat(part, axis):
    if lax.axis_size(axis) > 1:
        part = gather_half(part, 0, axis)
    return part


def gelu_parts(pre):
    square = pre * pre
    tanh = jnp.tanh(GELU_C * (pre + GELU_A * (square * pre)))
    half = 0.5 * (1.0 + tanh)
    slope = half + (0.5 * GELU_C) * pre * (1.0 - tanh * tanh) * (1.0 + (3.0 * GELU_A) * square)
    return pre * half, slope


def nt(a, b):
    return lax.dot_general(a, b, (((1,), (1,)), ((), ())), preferred_element_type=F32)


def tn(a, b):
    return lax.dot_general(a, b, (((0,), (0,)), ((), ())), preferred_element_type=F32)


def forward_kernel(sections, *refs):
    x = refs[:sections]
    bfly, low, lr_v, cot, act, d_pre, d_low = refs[sections : sections + 7]
    terms = refs[sections + 7 :]
    width = bfly.shape[2]
    tiles = bfly[0].reshape(sections * width, bfly.shape[3])
    block = jnp.concatenate([ref[...] for ref in x], axis=1)
    pre = jnp.dot(block, tiles, preferred_element_type=F32) + jnp.dot(
        low[...], lr_v[...], preferred_element_type=F32
    )
    value, slope = gelu_parts(pre)
    act[...] = value.astype(BF)
    grad = (cot[...].astype(F32) * slope).astype(BF)
    d_pre[...] = grad
    part = nt(grad, lr_v[...])

    @pl.when(pl.program_id(0) == 0)
    def _():
        d_low[...] = part

    @pl.when(pl.program_id(0) > 0)
    def _():
        d_low[...] += part

    back = nt(grad, tiles).astype(BF)
    for section in range(sections):
        terms[section][...] = back[:, section * width : (section + 1) * width]


def own_grad_kernel(sections, *refs):
    x = refs[:sections]
    low, d_pre, d_bfly, d_v = refs[sections:]
    block = jnp.concatenate([ref[...] for ref in x], axis=1)
    d_bfly[0] = tn(block, d_pre[...]).reshape(d_bfly.shape[1:])
    d_v[...] = tn(low[...], d_pre[...])


def other_grad_kernel(sections, scale, *refs):
    x = refs[:sections]
    bfly, low, lr_v, cot, d_bfly_in, d_v_in, d_bfly, d_v = refs[sections:]
    width = bfly.shape[2]
    tiles = bfly[0].reshape(sections * width, bfly.shape[3])
    block = jnp.concatenate([ref[...] for ref in x], axis=1)
    pre = jnp.dot(block, tiles, preferred_element_type=F32) + jnp.dot(
        low[...], lr_v[...], preferred_element_type=F32
    )
    _, slope = gelu_parts(pre)
    grad = (cot[...].astype(F32) * slope).astype(BF)
    d_bfly[0] = (d_bfly_in[0] + tn(block, grad).reshape(d_bfly.shape[1:])) * scale
    d_v[...] = (d_v_in[...] + tn(low[...], grad)) * scale


def column(rows, width, flip):
    return pl.BlockSpec((rows, width), lambda g: (0, g ^ flip))


def resident(*shape):
    return pl.BlockSpec(shape, lambda g: (0,) * len(shape))


def call(kernel, grid, in_specs, out_specs, out_shape, cost, aliases=None, name=None):
    return pl.pallas_call(
        kernel,
        grid=(grid,),
        in_specs=in_specs,
        out_specs=out_specs,
        out_shape=out_shape,
        input_output_aliases=aliases or {},
        cost_estimate=pl.CostEstimate(flops=cost[0], bytes_accessed=cost[1], transcendentals=0),
        compiler_params=pltpu.CompilerParams(vmem_limit_bytes=VMEM_LIMIT),
        name=name,
    )


def local(inputs, bfly, lr_u, lr_v, cotangent):
    tokens = inputs.shape[0]
    per_dev, sections, width, group = bfly.shape
    levels = sections - 1
    rank = lr_v.shape[0]
    local_bits = per_dev.bit_length() - 1
    data_groups = lax.axis_size("dp")
    scale = float(1.0 / np.sqrt(np.float32(tokens * data_groups)))
    remote = range(local_bits, levels)

    flips = [(1 << s) if s < local_bits else 0 for s in range(sections)]
    x_specs = [column(tokens, width, flip) for flip in flips]
    bfly_spec = pl.BlockSpec((1, sections, width, group), lambda g: (g, 0, 0, 0))
    low_spec = resident(tokens, rank)
    lr_v_spec = pl.BlockSpec((rank, group), lambda g: (0, g))
    wide_spec = column(tokens, group, 0)

    def fetch(block):
        got = {s: crossed(block, "feat", 1 << (s - local_bits)) for s in reversed(remote)}
        return [got.get(s, block) for s in range(sections)]

    low_part = jnp.dot(inputs, lr_u, preferred_element_type=F32)
    others = range(1, data_groups)
    x_others = [rolled(inputs, "dp", d) for d in others]
    partners = fetch(inputs)
    cot_others = [rolled(cotangent, "dp", d) for d in others]
    low_half = reduce_feat(low_part, "feat")
    low = finish_feat(low_half, "feat")
    low_others = [finish_feat(rolled(low_half, "dp", d), "feat") for d in others]
    partners_others = [fetch(x) for x in x_others]

    wide = jax.ShapeDtypeStruct((tokens, per_dev * group), BF)
    narrow = jax.ShapeDtypeStruct((tokens, per_dev * width), BF)
    unit = 2 * tokens * group * per_dev
    depth = sections * width
    out = call(
        functools.partial(forward_kernel, sections),
        per_dev,
        x_specs + [bfly_spec, low_spec, lr_v_spec, wide_spec],
        [wide_spec, wide_spec, resident(tokens, rank)] + x_specs,
        [wide, wide, jax.ShapeDtypeStruct((tokens, rank), F32)] + [narrow] * sections,
        (unit * 2 * (depth + rank), 20 * 2**20),
        name="forward",
    )(*partners, bfly, low, lr_v, cotangent)
    activated, d_pre, d_low_part = out[:3]
    terms = list(out[3:])
    for s in reversed(remote):
        terms[s] = crossed(terms[s], "feat", 1 << (s - local_bits))

    d_low_half = reduce_feat(d_low_part, "feat")
    d_low = finish_feat(d_low_half, "feat")
    d_low_others = [finish_feat(rolled(d_low_half, "dp", d), "feat") for d in others]

    tile_spec = bfly_spec
    tile_shape = jax.ShapeDtypeStruct(bfly.shape, F32)
    v_shape = jax.ShapeDtypeStruct(lr_v.shape, F32)
    d_bfly, d_v = call(
        functools.partial(own_grad_kernel, sections),
        per_dev,
        x_specs + [low_spec, wide_spec],
        [tile_spec, lr_v_spec],
        [tile_shape, v_shape],
        (unit * (depth + rank), 15 * 2**20),
        name="own_grad",
    )(*partners, low, d_pre)
    for d in others:
        last = scale if d == data_groups - 1 else 1.0
        d_bfly, d_v = call(
            functools.partial(other_grad_kernel, sections, last),
            per_dev,
            x_specs + [bfly_spec, low_spec, lr_v_spec, wide_spec, tile_spec, lr_v_spec],
            [tile_spec, lr_v_spec],
            [tile_shape, v_shape],
            (unit * 2 * (depth + rank), 30 * 2**20),
            aliases={sections + 4: 0, sections + 5: 1},
            name="other_grad",
        )(*partners_others[d - 1], bfly, low_others[d - 1], lr_v, cot_others[d - 1], d_bfly, d_v)
    if data_groups == 1:
        d_bfly, d_v = d_bfly * scale, d_v * scale

    d_inputs = nt(d_low, lr_u)
    for term in terms:
        d_inputs = d_inputs + term.astype(F32)
    d_u = tn(inputs, d_low)
    for d in others:
        d_u = d_u + tn(x_others[d - 1], d_low_others[d - 1])
    return activated, d_inputs.astype(BF), d_bfly, d_u * scale, d_v


def solution(mesh):
    return jax.shard_map(
        local,
        mesh=mesh,
        in_specs=(
            P("dp", "feat"),
            P("feat", None, None, None),
            P("feat", None),
            P(None, "feat"),
            P("dp", "feat"),
        ),
        out_specs=(
            P("dp", "feat"),
            P("dp", "feat"),
            P("feat", None, None, None),
            P("feat", None),
            P(None, "feat"),
        ),
        check_vma=False,
    )
```

```python
import functools

import jax
import jax.numpy as jnp
import numpy as np
from jax import lax
from jax.experimental import pallas as pl
from jax.experimental.pallas import tpu as pltpu
from jax.sharding import PartitionSpec as P

BF = jnp.bfloat16
F32 = jnp.float32
VMEM_LIMIT = 24 * 1024 * 1024
GELU_C = float(np.sqrt(2.0 / np.pi))
GELU_A = 0.044715


def crossed(block, axis, mask):
    count = lax.axis_size(axis)
    return lax.ppermute(block, axis, [(i, i ^ mask) for i in range(count)])


def rolled(block, axis, shift):
    count = lax.axis_size(axis)
    return lax.ppermute(block, axis, [(i, (i + shift) % count) for i in range(count)])


def scatter_half(part, bit, axis):
    rows = part.shape[0] // 2
    mine = (lax.axis_index(axis) >> bit) & 1
    keep = lax.dynamic_slice_in_dim(part, mine * rows, rows, 0)
    send = lax.dynamic_slice_in_dim(part, (1 - mine) * rows, rows, 0)
    return keep + crossed(send.astype(BF), axis, 1 << bit).astype(F32)


def gather_half(part, bit, axis):
    mine = (lax.axis_index(axis) >> bit) & 1
    other = crossed(part, axis, 1 << bit)
    low = jnp.where(mine == 0, part, other)
    high = jnp.where(mine == 0, other, part)
    return jnp.concatenate([low, high], 0)


def tie(value, *others):
    return lax.optimization_barrier((value, *others))


def no_hooks(step, value):
    return value


def reduce_feat(part, axis, hooks):
    bits = lax.axis_size(axis).bit_length() - 1
    near = min(bits, 2)
    for bit in range(near):
        part = hooks(f"scatter{bit}", scatter_half(part, bit, axis))
    for bit in range(near, bits):
        got = hooks(f"got{bits - 1 - bit}", crossed(part.astype(BF), axis, 1 << bit))
        part = hooks(f"far{bits - 1 - bit}", part + got.astype(F32))
    return part.astype(BF)


def gather_feat(part, axis, hooks=no_hooks):
    near = min(lax.axis_size(axis).bit_length() - 1, 2)
    for bit in range(near - 1, -1, -1):
        part = hooks(f"gather{bit}", gather_half(part, bit, axis))
    return part


def gelu_parts(pre):
    square = pre * pre
    tanh = jnp.tanh(GELU_C * (pre + GELU_A * (square * pre)))
    half = 0.5 * (1.0 + tanh)
    slope = half + (0.5 * GELU_C) * pre * (1.0 - tanh * tanh) * (1.0 + (3.0 * GELU_A) * square)
    return pre * half, slope


def nt(a, b):
    return lax.dot_general(a, b, (((1,), (1,)), ((), ())), preferred_element_type=F32)


def tn(a, b):
    return lax.dot_general(a, b, (((0,), (0,)), ((), ())), preferred_element_type=F32)


def gathered(refs, pieces):
    refs = iter(refs)
    columns = []
    for count in pieces:
        rows = [next(refs)[...] for _ in range(count)]
        columns.append(rows[0] if count == 1 else jnp.concatenate(rows, axis=0))
    return columns[0] if len(columns) == 1 else jnp.concatenate(columns, axis=1)


def forward_kernel(pieces, *refs):
    sections, count = len(pieces), sum(pieces)
    x = refs[:count]
    bfly, low, lr_v, cot, act, d_pre, d_low = refs[count : count + 7]
    terms = refs[count + 7 :]
    width = bfly.shape[2]
    tiles = bfly[0].reshape(sections * width, bfly.shape[3])
    block = gathered(x, pieces)
    pre = jnp.dot(block, tiles, preferred_element_type=F32) + jnp.dot(
        low[...], lr_v[...], preferred_element_type=F32
    )
    value, slope = gelu_parts(pre)
    act[...] = value.astype(BF)
    grad = (cot[...].astype(F32) * slope).astype(BF)
    d_pre[...] = grad
    part = nt(grad, lr_v[...])

    @pl.when(pl.program_id(0) == 0)
    def _():
        d_low[...] = part

    @pl.when(pl.program_id(0) > 0)
    def _():
        d_low[...] += part

    back = nt(grad, tiles).astype(BF)
    for section in range(sections):
        terms[section][...] = back[:, section * width : (section + 1) * width]


def own_grad_kernel(pieces, *refs):
    count = sum(pieces)
    x = refs[:count]
    low, d_pre, d_bfly, d_v = refs[count:]
    block = gathered(x, pieces)
    d_bfly[0] = tn(block, d_pre[...]).reshape(d_bfly.shape[1:])
    d_v[...] = tn(low[...], d_pre[...])


def other_grad_kernel(pieces, scale, *refs):
    sections, count = len(pieces), sum(pieces)
    x = refs[:count]
    bfly, low, lr_v, cot, d_bfly_in, d_v_in, d_bfly, d_v = refs[count:]
    width = bfly.shape[2]
    tiles = bfly[0].reshape(sections * width, bfly.shape[3])
    block = gathered(x, pieces)
    pre = jnp.dot(block, tiles, preferred_element_type=F32) + jnp.dot(
        low[...], lr_v[...], preferred_element_type=F32
    )
    _, slope = gelu_parts(pre)
    grad = (cot[...].astype(F32) * slope).astype(BF)
    d_bfly[0] = (d_bfly_in[0] + tn(block, grad).reshape(d_bfly.shape[1:])) * scale
    d_v[...] = (d_v_in[...] + tn(low[...], grad)) * scale


def column(rows, width, flip, base=0):
    return pl.BlockSpec((rows, width), lambda g: (0, (g + base) ^ flip))


def row(rows, width, base=0):
    return pl.BlockSpec((rows, width), lambda g: (0, g + base))


def resident(*shape):
    return pl.BlockSpec(shape, lambda g: (0,) * len(shape))


def call(kernel, grid, in_specs, out_specs, out_shape, cost, aliases=None, name=None):
    return pl.pallas_call(
        kernel,
        grid=(grid,),
        in_specs=in_specs,
        out_specs=out_specs,
        out_shape=out_shape,
        input_output_aliases=aliases or {},
        cost_estimate=pl.CostEstimate(flops=cost[0], bytes_accessed=cost[1], transcendentals=0),
        compiler_params=pltpu.CompilerParams(vmem_limit_bytes=VMEM_LIMIT),
        name=name,
    )


def local(inputs, bfly, lr_u, lr_v, cotangent):
    tokens = inputs.shape[0]
    per_dev, sections, width, group = bfly.shape
    levels = sections - 1
    rank = lr_v.shape[0]
    local_bits = per_dev.bit_length() - 1
    data_groups = lax.axis_size("dp")
    scale = float(1.0 / np.sqrt(np.float32(tokens * data_groups)))
    remote = list(range(local_bits, levels))
    others = range(1, data_groups)

    flips = [(1 << s) if s < local_bits else 0 for s in range(sections)]

    def tile_spec(base=0):
        return pl.BlockSpec((1, sections, width, group), lambda g: (g + base, 0, 0, 0))

    low_spec = resident(tokens, rank)
    wide = jax.ShapeDtypeStruct((tokens, per_dev * group), BF)
    narrow = jax.ShapeDtypeStruct((tokens, per_dev * width), BF)
    tile_shape = jax.ShapeDtypeStruct(bfly.shape, F32)
    v_shape = jax.ShapeDtypeStruct(lr_v.shape, F32)

    def to_partner(block, section):
        return crossed(block, "feat", 1 << (section - local_bits))

    env = {}
    seen = set()

    def pin(value, *names):
        names = [n for n in names if n in env]
        if names:
            value, *rest = tie(value, *[env[n] for n in names])
            env.update(zip(names, rest))
        return value

    def each(prefix, *tails):
        return [f"{prefix}{d}{t}" for d in others for t in tails or ("",)]

    far = remote[-1:]
    near = remote[:-1]
    lead = 1
    parts = [(0, lead), (lead, per_dev)] if per_dev > lead else [(0, lead)]

    low_part = jnp.dot(inputs, lr_u, preferred_element_type=F32)
    for s in reversed(near[1:] + far):
        env[f"x{s}"] = to_partner(inputs, s)
    joined = jnp.concatenate([cotangent[:, : lead * group], inputs], axis=1)
    for d in others:
        env[f"in{d}"] = rolled(joined, "dp", d)

    def send_cot(value, index):
        first, last = parts[index]
        piece = tie(cotangent[:, first * group : last * group], value)[0]
        for d in others:
            env[f"cot{d}{index}"] = rolled(piece, "dp", d)

    def low_hooks(step, value):
        if step == "scatter1":
            value = pin(value, *[f"x{s}" for s in near[1:] + far])
        if step == "far0":
            value = pin(value, *each("in"))
        return value

    low = reduce_feat(low_part, "feat", low_hooks)
    for s in near[:1]:
        env[f"x{s}"] = to_partner(tie(inputs, low)[0], s)
    for d in others:
        env[f"low{d}"] = rolled(low, "dp", d)
    low = gather_feat(low, "feat")
    for d in others:
        env[f"cot{d}0"] = env[f"in{d}"]
        env[f"in{d}"] = env[f"in{d}"][:, lead * group :]
        for s in near:
            env[f"xo{d}{s}"] = to_partner(env[f"in{d}"], s)
        for s in far:
            env[f"xo{d}{s}"] = rolled(env[f"x{s}"], "dp", d)
    for index in range(1, len(parts)):
        send_cot(env["low1"] if others else low, index)
    low = pin(low, *[f"x{s}" for s in remote])

    def x_blocks(base_block, prefix, base):
        arrays = [env.get(f"{prefix}{s}", base_block) for s in range(sections)]
        return arrays, [column(tokens, width, flip, base) for flip in flips]

    arrays, specs = x_blocks(inputs, "x", 0)
    term_specs = [column(tokens, width, flip) for flip in flips]
    out = call(
        functools.partial(forward_kernel, [1] * sections),
        per_dev,
        specs + [tile_spec(), low_spec, row(rank, group), row(tokens, group)],
        [row(tokens, group), row(tokens, group), resident(tokens, rank)] + term_specs,
        [wide, wide, jax.ShapeDtypeStruct((tokens, rank), F32)] + [narrow] * sections,
        (1000, 1000),
        name="forward",
    )(*arrays, bfly, low, lr_v, cotangent)
    activated, d_pre, d_low_part = out[:3]
    terms = list(out[3:])
    for s in reversed(near[2:] + far):
        env[f"t{s}"] = to_partner(terms[s], s)
    grads = []

    def own_grad(gate):
        d_bfly, env["own"] = call(
            functools.partial(own_grad_kernel, [1] * sections),
            per_dev,
            specs + [low_spec, row(tokens, group)],
            [tile_spec(), row(rank, group)],
            [tile_shape, v_shape],
            (1000, 1000),
            name="own_grad",
        )(*arrays, low, tie(d_pre, gate)[0])
        grads.append(d_bfly)

    def add_other(d, index):
        base, end = parts[index]
        last = scale if d == data_groups - 1 else 1.0
        arrays, specs = x_blocks(env[f"in{d}"], f"xo{d}", base)
        count = len(arrays) + 4
        grads[0], env["own"] = call(
            functools.partial(other_grad_kernel, [1] * sections, last),
            end - base,
            specs
            + [tile_spec(base), low_spec, row(rank, group, base), row(tokens, group)]
            + [tile_spec(base), row(rank, group, base)],
            [tile_spec(base), row(rank, group, base)],
            [tile_shape, v_shape],
            (1000, 1000),
            aliases={count: 0, count + 1: 1},
            name="other_grad",
        )(*arrays, bfly, env[f"low{d}"], lr_v, env[f"cot{d}{index}"], grads[0], env["own"])

    def d_low_hooks(step, value):
        seen.add(step)
        if step == "scatter0":
            value = pin(value, *each("xo", *near))
            own_grad(value)
            for d in others:
                env[f"low{d}"] = gather_feat(tie(env[f"low{d}"], value)[0], "feat")
            value = pin(value, *each("cot", 1))
        if step == "scatter1":
            for s in near[1:2]:
                env[f"t{s}"] = to_partner(tie(terms[s], value)[0], s)
            for d in others:
                for index in range(len(parts)):
                    add_other(d, index)
            value = pin(value, "own", *[f"t{s}" for s in near[2:] + far])
        if step == "got0":
            value = pin(value, *[f"t{s}" for s in near[1:2]])
        return value

    d_low = reduce_feat(d_low_part, "feat", d_low_hooks)
    d_low_others = [gather_feat(rolled(d_low, "dp", d), "feat") for d in others]
    d_low = gather_feat(d_low, "feat", d_low_hooks)
    if not grads:
        own_grad(d_low)
    if "scatter1" not in seen:
        for d in others:
            for index in range(len(parts)):
                add_other(d, index)
    d_bfly, d_v = grads[0], env["own"]
    if data_groups == 1:
        d_bfly, d_v = d_bfly * scale, d_v * scale

    for s in near[:1]:
        env[f"t{s}"] = to_partner(terms[s], s)
    d_inputs = nt(d_low, lr_u)
    for s in range(sections):
        d_inputs = d_inputs + env.get(f"t{s}", terms[s]).astype(F32)
    d_u = tn(inputs, d_low)
    for d in others:
        d_u = d_u + tn(env[f"in{d}"], d_low_others[d - 1])
    return activated, d_inputs.astype(BF), d_bfly, d_u * scale, d_v


def solution(mesh):
    return jax.shard_map(
        local,
        mesh=mesh,
        in_specs=(
            P("dp", "feat"),
            P("feat", None, None, None),
            P("feat", None),
            P(None, "feat"),
            P("dp", "feat"),
        ),
        out_specs=(
            P("dp", "feat"),
            P("dp", "feat"),
            P("feat", None, None, None),
            P("feat", None),
            P(None, "feat"),
        ),
        check_vma=False,
    )
```

```python
import functools

import jax
import jax.numpy as jnp
import numpy as np
from jax import lax
from jax.experimental import pallas as pl
from jax.experimental.pallas import tpu as pltpu
from jax.sharding import PartitionSpec as P

BF = jnp.bfloat16
F32 = jnp.float32
VMEM_LIMIT = 32 * 1024 * 1024
GELU_C = float(np.sqrt(2.0 / np.pi))
GELU_A = 0.044715


def crossed(block, axis, mask):
    count = lax.axis_size(axis)
    return lax.ppermute(block, axis, [(i, i ^ mask) for i in range(count)])


def rolled(block, axis, shift):
    count = lax.axis_size(axis)
    return lax.ppermute(block, axis, [(i, (i + shift) % count) for i in range(count)])


def scatter_half(part, bit, axis):
    rows = part.shape[0] // 2
    mine = (lax.axis_index(axis) >> bit) & 1
    keep = lax.dynamic_slice_in_dim(part, mine * rows, rows, 0)
    send = lax.dynamic_slice_in_dim(part, (1 - mine) * rows, rows, 0)
    return keep + crossed(send.astype(BF), axis, 1 << bit).astype(F32)


def tie(value, *others):
    return lax.optimization_barrier((value, *others))


def no_hooks(step, value):
    return value


def near_bits(axis):
    return min(lax.axis_size(axis).bit_length() - 1, 2)


def scatter_near(part, axis, hooks, direct):
    near = near_bits(axis)
    if not direct:
        for bit in range(near):
            part = hooks(f"scatter{bit}", scatter_half(part, bit, axis))
        return part
    count = 1 << near
    rows = part.shape[0] // count
    mine = lax.axis_index(axis) & (count - 1)
    total = lax.dynamic_slice_in_dim(part, mine * rows, rows, 0)
    for mask in range(1, count):
        send = lax.dynamic_slice_in_dim(part, (mine ^ mask) * rows, rows, 0)
        total = total + crossed(send.astype(BF), axis, mask).astype(F32)
    return hooks("scatter", total)


def sum_far(part, axis, hooks):
    near = near_bits(axis)
    sent = part.astype(BF)
    for mask in range(1, lax.axis_size(axis) >> near):
        part = part + crossed(sent, axis, mask << near).astype(F32)
    return hooks("far", part).astype(BF)


def gather_near(part, axis, direct):
    near = near_bits(axis)
    mine = lax.axis_index(axis)
    held = [part] + [crossed(part, axis, mask) for mask in range(1, 1 << near)]
    for bit in range(near):
        swap = (mine >> bit) & 1
        held = [jnp.where(swap == 0, h, held[i ^ (1 << bit)]) for i, h in enumerate(held)]
    if not direct and near == 2:
        held = [held[i] for i in (0, 2, 1, 3)]
    return jnp.concatenate(held, 0)


def gelu_parts(pre):
    square = pre * pre
    tanh = jnp.tanh(GELU_C * (pre + GELU_A * (square * pre)))
    half = 0.5 * (1.0 + tanh)
    slope = half + (0.5 * GELU_C) * pre * (1.0 - tanh * tanh) * (1.0 + (3.0 * GELU_A) * square)
    return pre * half, slope


def nt(a, b):
    return lax.dot_general(a, b, (((1,), (1,)), ((), ())), preferred_element_type=F32)


def tn(a, b):
    return lax.dot_general(a, b, (((0,), (0,)), ((), ())), preferred_element_type=F32)


def gathered(refs, pieces):
    refs = iter(refs)
    columns = []
    for count in pieces:
        rows = [next(refs)[...] for _ in range(count)]
        columns.append(rows[0] if count == 1 else jnp.concatenate(rows, axis=0))
    return columns[0] if len(columns) == 1 else jnp.concatenate(columns, axis=1)


def forward_kernel(pieces, *refs):
    sections, count = len(pieces), sum(pieces)
    x = refs[:count]
    bfly, low, lr_v, cot, act, d_pre, d_low = refs[count : count + 7]
    terms = refs[count + 7 :]
    width = bfly.shape[2]
    tiles = bfly[0].reshape(sections * width, bfly.shape[3])
    block = gathered(x, pieces)
    pre = jnp.dot(block, tiles, preferred_element_type=F32) + jnp.dot(
        low[...], lr_v[...], preferred_element_type=F32
    )
    value, slope = gelu_parts(pre)
    act[...] = value.astype(BF)
    grad = (cot[...].astype(F32) * slope).astype(BF)
    d_pre[...] = grad
    part = nt(grad, lr_v[...])

    @pl.when(pl.program_id(0) == 0)
    def _():
        d_low[...] = part

    @pl.when(pl.program_id(0) > 0)
    def _():
        d_low[...] += part

    back = nt(grad, tiles).astype(BF)
    for section in range(sections):
        terms[section][...] = back[:, section * width : (section + 1) * width]


def weight_grad_kernel(sections, own, other, starts, scale, *refs):
    refs = list(refs)

    def take(count):
        taken, refs[:] = refs[:count], refs[count:]
        return taken

    def side(x):
        return jnp.concatenate([ref[...] for ref in x], axis=1)

    parts = []
    if own:
        block = side(take(sections))
        low, grad = (ref[...] for ref in take(2))
        parts.append((tn(block, grad), tn(low, grad)))
    if other:
        block = side(take(sections))
        bfly, low, lr_v = take(3)
        cots = take(len(starts))
        cot = cots[0][...]
        for start, piece in zip(starts[1:], cots[1:]):
            cot = jnp.where(pl.program_id(0) >= start, piece[...], cot)
        tiles = bfly[0].reshape(sections * bfly.shape[2], bfly.shape[3])
        pre = jnp.dot(block, tiles, preferred_element_type=F32) + jnp.dot(
            low[...], lr_v[...], preferred_element_type=F32
        )
        _, slope = gelu_parts(pre)
        grad = (cot.astype(F32) * slope).astype(BF)
        parts.append((tn(block, grad), tn(low[...], grad)))
    if not own:
        d_bfly_in, d_v_in = take(2)
        parts.append((d_bfly_in[0].reshape(parts[0][0].shape), d_v_in[...]))
    d_bfly, d_v = refs
    total, total_v = parts[0]
    for part, part_v in parts[1:]:
        total, total_v = total + part, total_v + part_v
    d_bfly[0] = (total * scale).reshape(d_bfly.shape[1:])
    d_v[...] = total_v * scale


def finish_kernel(sections, others, scale, *refs):
    terms, (d_low, lr_u, x), rest = refs[:sections], refs[sections : sections + 3], refs[sections + 3 :]
    d_inputs, d_u = rest[2 * others :]
    total = nt(d_low[...], lr_u[...])
    for term in terms:
        total = total + term[...].astype(F32)
    d_inputs[...] = total.astype(BF)
    grad = tn(x[...], d_low[...])
    for other in range(others):
        grad = grad + tn(rest[2 * other][...], rest[2 * other + 1][...])
    d_u[...] = grad * scale


def column(rows, width, flip, base=0, at=0):
    return pl.BlockSpec((rows, width), lambda g: (at, (g + base) ^ flip))


def row(rows, width, base=0, at=0):
    return pl.BlockSpec((rows, width), lambda g: (at, g + base))


def clipped(rows, width, start, count):
    return pl.BlockSpec((rows, width), lambda g: (0, jnp.clip(g - start, 0, count - 1)))


def in_hbm(array):
    return pltpu.with_memory_space_constraint(array, pltpu.HBM)


def resident(*shape):
    return pl.BlockSpec(shape, lambda g: (0,) * len(shape))


def call(kernel, grid, in_specs, out_specs, out_shape, cost, aliases=None, name=None):
    return pl.pallas_call(
        kernel,
        grid=(grid,),
        in_specs=in_specs,
        out_specs=out_specs,
        out_shape=out_shape,
        input_output_aliases=aliases or {},
        cost_estimate=pl.CostEstimate(flops=cost[0], bytes_accessed=cost[1], transcendentals=0),
        compiler_params=pltpu.CompilerParams(vmem_limit_bytes=VMEM_LIMIT),
        name=name,
    )


def local(inputs, bfly, lr_u, lr_v, cotangent):
    tokens = inputs.shape[0]
    per_dev, sections, width, group = bfly.shape
    levels = sections - 1
    rank = lr_v.shape[0]
    local_bits = per_dev.bit_length() - 1
    data_groups = lax.axis_size("dp")
    scale = float(1.0 / np.sqrt(np.float32(tokens * data_groups)))
    remote = list(range(local_bits, levels))
    others = range(1, data_groups)

    flips = [(1 << s) if s < local_bits else 0 for s in range(sections)]

    def tile_spec(base=0):
        return pl.BlockSpec((1, sections, width, group), lambda g: (g + base, 0, 0, 0))

    low_spec = resident(tokens, rank)
    wide = jax.ShapeDtypeStruct((tokens, per_dev * group), BF)
    narrow = jax.ShapeDtypeStruct((tokens, per_dev * width), BF)
    tile_shape = jax.ShapeDtypeStruct(bfly.shape, F32)
    v_shape = jax.ShapeDtypeStruct(lr_v.shape, F32)

    def to_partner(block, section):
        return crossed(block, "feat", 1 << (section - local_bits))

    env = {}

    def pin(value, *names):
        names = [n for n in names if n in env]
        if names:
            value, *rest = tie(value, *[env[n] for n in names])
            env.update(zip(names, rest))
        return value

    def each(prefix, *tails):
        return [f"{prefix}{d}{t}" for d in others for t in tails or ("",)]

    far = remote[-1:]
    near = remote[:-1]
    lead = 1
    parts = [(0, lead), (lead, per_dev)] if per_dev > lead else [(0, lead)]

    low_part = jnp.dot(inputs, lr_u, preferred_element_type=F32)
    for s in reversed(near[1:] + far):
        env[f"x{s}"] = to_partner(inputs, s)
    joined = jnp.concatenate([cotangent[:, : lead * group], inputs], axis=1)
    for d in others:
        env[f"in{d}"] = rolled(joined, "dp", d)

    def cut_rest():
        pieces = [cotangent[:, lead * group :]] if per_dev > lead else []
        pieces += [env[f"x{s}"] for s in far]
        env["cut"] = jnp.concatenate(pieces, axis=1) if len(pieces) > 1 else pieces[0]

    def send_rest(value):
        piece = tie(env["cut"], value)[0]
        for d in others:
            env[f"rest{d}"] = rolled(piece, "dp", d)

    def low_hooks(step, value):
        if step == "scatter1":
            value = pin(value, *[f"x{s}" for s in near[1:] + far])
            cut_rest()
        if step == "far":
            value = pin(value, *each("in"), "cut")
        return value

    low = sum_far(scatter_near(low_part, "feat", low_hooks, False), "feat", low_hooks)
    for s in near[:1]:
        env[f"x{s}"] = to_partner(tie(inputs, low)[0], s)
    for d in others:
        env[f"low{d}"] = rolled(low, "dp", d)
    low = gather_near(low, "feat", False)
    for d in others:
        env[f"cot{d}0"] = env[f"in{d}"]
        env[f"in{d}"] = env[f"in{d}"][:, lead * group :]
        for s in near[1:]:
            env[f"xo{d}{s}"] = to_partner(tie(env[f"in{d}"], low)[0], s)
    send_rest(env["low1"] if others else low)
    low = pin(low, *[f"x{s}" for s in remote])

    def x_blocks(base_block, prefix):
        arrays = [env.get(f"{prefix}{s}", base_block) for s in range(sections)]
        return arrays, [column(tokens, width, flip) for flip in flips]

    arrays, specs = x_blocks(inputs, "x")
    term_specs = [column(tokens, width, flip) for flip in flips]
    out = call(
        functools.partial(forward_kernel, [1] * sections),
        per_dev,
        specs + [tile_spec(), low_spec, row(rank, group), row(tokens, group)],
        [row(tokens, group), row(tokens, group), resident(tokens, rank)] + term_specs,
        [wide, wide, jax.ShapeDtypeStruct((tokens, rank), F32)]
        + [pltpu.HBM(narrow.shape, BF)] * sections,
        (1000, 1000),
        name="forward",
    )(*arrays, in_hbm(bfly), low, lr_v, in_hbm(cotangent))
    activated, d_pre, d_low_part = out[:3]
    terms = list(out[3:])
    for d in others:
        env[f"low{d}"] = gather_near(tie(env[f"low{d}"], d_low_part)[0], "feat", False)

    def send_terms(value, which):
        for s in reversed(which):
            env[f"t{s}"] = to_partner(tie(terms[s], value)[0], s)

    def d_low_hooks(step, value):
        if step == "scatter":
            for d in others:
                for s in near[:1]:
                    env[f"xo{d}{s}"] = to_partner(tie(env[f"in{d}"], value)[0], s)
        if step == "far":
            send_terms(value, near[1:] + far)
        return value

    d_low_part = pin(d_low_part, *each("xo", *near[1:]))
    d_low = sum_far(scatter_near(d_low_part, "feat", d_low_hooks, True), "feat", d_low_hooks)
    d_low = gather_near(d_low, "feat", True)
    for d in others:
        env[f"d_low{d}"] = rolled(d_low, "dp", d)

    grads = []
    for d in [0, *others] if data_groups == 1 or data_groups > 2 else [1]:
        own, other = d == 0 or data_groups == 2, d > 0
        last = scale if d == data_groups - 1 else 1.0
        operands, blocks = [], []
        if own:
            operands += arrays + [low, d_pre]
            blocks += specs + [low_spec, row(tokens, group)]
        if other:
            x_others, x_specs = x_blocks(env[f"in{d}"], f"xo{d}")
            for s in far:
                x_others[s] = env[f"rest{d}"]
                x_specs[s] = column(tokens, width, 0, (per_dev - lead) * group // width)
            cots = [in_hbm(a) for a in (env[f"cot{d}0"], env[f"rest{d}"])[: len(parts)]]
            operands += x_others + [in_hbm(bfly), env[f"low{d}"], lr_v] + cots
            blocks += x_specs + [tile_spec(), low_spec, row(rank, group)]
            blocks += [clipped(tokens, group, p[0], p[1] - p[0]) for p in parts]
        count = len(operands)
        grads = call(
            functools.partial(
                weight_grad_kernel, sections, own, other, [p[0] for p in parts], last
            ),
            per_dev,
            blocks + ([tile_spec(), row(rank, group)] if grads else []),
            [tile_spec(), row(rank, group)],
            [tile_shape, v_shape],
            (1000, 1000),
            aliases={count: 0, count + 1: 1} if grads else None,
            name="weight_grad",
        )(*operands, *grads)
    d_bfly, d_v = grads

    send_terms(d_low, [s for s in remote if f"t{s}" not in env])
    d_low, d_v = tie(d_low, d_v)
    last_arrays = [env.get(f"t{s}", terms[s]) for s in range(sections)] + [d_low, lr_u, inputs]
    for d in others:
        last_arrays += [env[f"in{d}"], env[f"d_low{d}"]]
    d_inputs, d_u = call(
        functools.partial(finish_kernel, sections, data_groups - 1, scale),
        1,
        [resident(*a.shape) for a in last_arrays],
        [resident(*narrow.shape), resident(*lr_u.shape)],
        [narrow, jax.ShapeDtypeStruct(lr_u.shape, F32)],
        (1000, 1000),
        name="finish",
    )(*last_arrays)
    return activated, d_inputs, d_bfly, d_u, d_v


def solution(mesh):
    return jax.shard_map(
        local,
        mesh=mesh,
        in_specs=(
            P("dp", "feat"),
            P("feat", None, None, None),
            P("feat", None),
            P(None, "feat"),
            P("dp", "feat"),
        ),
        out_specs=(
            P("dp", "feat"),
            P("dp", "feat"),
            P("feat", None, None, None),
            P("feat", None),
            P(None, "feat"),
        ),
        check_vma=False,
    )
```

```python
import functools

import jax
import jax.numpy as jnp
import numpy as np
from jax import lax
from jax.experimental import pallas as pl
from jax.experimental.pallas import tpu as pltpu
from jax.sharding import PartitionSpec as P

BF = jnp.bfloat16
F32 = jnp.float32
VMEM_LIMIT = 32 * 1024 * 1024
GELU_C = float(np.sqrt(2.0 / np.pi))
GELU_A = 0.044715


def crossed(block, axis, mask):
    count = lax.axis_size(axis)
    return lax.ppermute(block, axis, [(i, i ^ mask) for i in range(count)])


def rolled(block, axis, shift):
    count = lax.axis_size(axis)
    return lax.ppermute(block, axis, [(i, (i + shift) % count) for i in range(count)])


def scatter_half(part, bit, axis):
    rows = part.shape[0] // 2
    mine = (lax.axis_index(axis) >> bit) & 1
    keep = lax.dynamic_slice_in_dim(part, mine * rows, rows, 0)
    send = lax.dynamic_slice_in_dim(part, (1 - mine) * rows, rows, 0)
    return keep + crossed(send.astype(BF), axis, 1 << bit).astype(F32)


def tie(value, *others):
    return lax.optimization_barrier((value, *others))


def no_hooks(step, value):
    return value


def near_bits(axis):
    return min(lax.axis_size(axis).bit_length() - 1, 2)


def scatter_near(part, axis, hooks, direct):
    near = near_bits(axis)
    if not direct:
        for bit in range(near):
            part = hooks(f"scatter{bit}", scatter_half(part, bit, axis))
        return part
    count = 1 << near
    rows = part.shape[0] // count
    mine = lax.axis_index(axis) & (count - 1)
    total = lax.dynamic_slice_in_dim(part, mine * rows, rows, 0)
    for mask in range(1, count):
        send = lax.dynamic_slice_in_dim(part, (mine ^ mask) * rows, rows, 0)
        total = total + crossed(send.astype(BF), axis, mask).astype(F32)
    return hooks("scatter", total)


def sum_far(part, axis, hooks):
    near = near_bits(axis)
    sent = part.astype(BF)
    for mask in range(1, lax.axis_size(axis) >> near):
        part = part + crossed(sent, axis, mask << near).astype(F32)
    return hooks("far", part).astype(BF)


def gather_near(part, axis, direct):
    near = near_bits(axis)
    mine = lax.axis_index(axis)
    held = [part] + [crossed(part, axis, mask) for mask in range(1, 1 << near)]
    for bit in range(near):
        swap = (mine >> bit) & 1
        held = [jnp.where(swap == 0, h, held[i ^ (1 << bit)]) for i, h in enumerate(held)]
    if not direct and near == 2:
        held = [held[i] for i in (0, 2, 1, 3)]
    return jnp.concatenate(held, 0)


def gelu_parts(pre):
    square = pre * pre
    tanh = jnp.tanh(GELU_C * (pre + GELU_A * (square * pre)))
    half = 0.5 * (1.0 + tanh)
    slope = half + (0.5 * GELU_C) * pre * (1.0 - tanh * tanh) * (1.0 + (3.0 * GELU_A) * square)
    return pre * half, slope


def nt(a, b):
    return lax.dot_general(a, b, (((1,), (1,)), ((), ())), preferred_element_type=F32)


def tn(a, b):
    return lax.dot_general(a, b, (((0,), (0,)), ((), ())), preferred_element_type=F32)


def gathered(refs, pieces):
    refs = iter(refs)
    columns = []
    for count in pieces:
        rows = [next(refs)[...] for _ in range(count)]
        columns.append(rows[0] if count == 1 else jnp.concatenate(rows, axis=0))
    return columns[0] if len(columns) == 1 else jnp.concatenate(columns, axis=1)


def forward_kernel(pieces, *refs):
    sections, count = len(pieces), sum(pieces)
    x = refs[:count]
    bfly, low, lr_v, cot, act, d_pre, d_low = refs[count : count + 7]
    terms = refs[count + 7 :]
    width = bfly.shape[2]
    tiles = bfly[0].reshape(sections * width, bfly.shape[3])
    block = gathered(x, pieces)
    pre = jnp.dot(block, tiles, preferred_element_type=F32) + jnp.dot(
        low[...], lr_v[...], preferred_element_type=F32
    )
    value, slope = gelu_parts(pre)
    act[...] = value.astype(BF)
    grad = (cot[...].astype(F32) * slope).astype(BF)
    d_pre[...] = grad
    part = nt(grad, lr_v[...])

    @pl.when(pl.program_id(0) == 0)
    def _():
        d_low[...] = part

    @pl.when(pl.program_id(0) > 0)
    def _():
        d_low[...] += part

    back = nt(grad, tiles).astype(BF)
    for section in range(sections):
        terms[section][...] = back[:, section * width : (section + 1) * width]


def weight_grad_kernel(sections, own, other, starts, scale, *refs):
    refs = list(refs)

    def take(count):
        taken, refs[:] = refs[:count], refs[count:]
        return taken

    def side(x):
        return jnp.concatenate([ref[...] for ref in x], axis=1)

    blocks, lows, grads = [], [], []
    if own:
        blocks.append(side(take(sections)))
        low, grad = take(2)
        lows.append(low[...])
        grads.append(grad[...])
    if other:
        block = side(take(sections))
        bfly, low, lr_v = take(3)
        cots = take(len(starts))
        cot = cots[0][...]
        for start, piece in zip(starts[1:], cots[1:]):
            cot = jnp.where(pl.program_id(0) >= start, piece[...], cot)
        tiles = bfly[0].reshape(sections * bfly.shape[2], bfly.shape[3])
        pre = jnp.dot(block, tiles, preferred_element_type=F32) + jnp.dot(
            low[...], lr_v[...], preferred_element_type=F32
        )
        _, slope = gelu_parts(pre)
        blocks.append(block)
        lows.append(low[...])
        grads.append((cot.astype(F32) * slope).astype(BF))
    block, low, grad = (
        a[0] if len(a) == 1 else jnp.concatenate(a, axis=0) for a in (blocks, lows, grads)
    )
    total, total_v = tn(block, grad), tn(low, grad)
    if not own:
        d_bfly_in, d_v_in = take(2)
        total = total + d_bfly_in[0].reshape(total.shape)
        total_v = total_v + d_v_in[...]
    d_bfly, d_v = refs
    d_bfly[0] = (total * scale).reshape(d_bfly.shape[1:])
    d_v[...] = total_v * scale


def finish_kernel(sections, others, scale, *refs):
    terms, (d_low, lr_u, x), rest = refs[:sections], refs[sections : sections + 3], refs[sections + 3 :]
    d_inputs, d_u = rest[2 * others :]
    total = nt(d_low[...], lr_u[...])
    for term in terms:
        total = total + term[...].astype(F32)
    d_inputs[...] = total.astype(BF)
    grad = tn(x[...], d_low[...])
    for other in range(others):
        grad = grad + tn(rest[2 * other][...], rest[2 * other + 1][...])
    d_u[...] = grad * scale


def column(rows, width, flip, base=0, at=0):
    return pl.BlockSpec((rows, width), lambda g: (at, (g + base) ^ flip))


def row(rows, width, base=0, at=0):
    return pl.BlockSpec((rows, width), lambda g: (at, g + base))


def clipped(rows, width, start, count):
    return pl.BlockSpec((rows, width), lambda g: (0, jnp.clip(g - start, 0, count - 1)))


def in_hbm(array):
    return pltpu.with_memory_space_constraint(array, pltpu.HBM)


def resident(*shape):
    return pl.BlockSpec(shape, lambda g: (0,) * len(shape))


def call(kernel, grid, in_specs, out_specs, out_shape, cost, aliases=None, name=None):
    return pl.pallas_call(
        kernel,
        grid=(grid,),
        in_specs=in_specs,
        out_specs=out_specs,
        out_shape=out_shape,
        input_output_aliases=aliases or {},
        cost_estimate=pl.CostEstimate(flops=cost[0], bytes_accessed=cost[1], transcendentals=0),
        compiler_params=pltpu.CompilerParams(vmem_limit_bytes=VMEM_LIMIT),
        name=name,
    )


def local(inputs, bfly, lr_u, lr_v, cotangent):
    tokens = inputs.shape[0]
    per_dev, sections, width, group = bfly.shape
    levels = sections - 1
    rank = lr_v.shape[0]
    local_bits = per_dev.bit_length() - 1
    data_groups = lax.axis_size("dp")
    scale = float(1.0 / np.sqrt(np.float32(tokens * data_groups)))
    remote = list(range(local_bits, levels))
    others = range(1, data_groups)

    flips = [(1 << s) if s < local_bits else 0 for s in range(sections)]

    def tile_spec(base=0):
        return pl.BlockSpec((1, sections, width, group), lambda g: (g + base, 0, 0, 0))

    low_spec = resident(tokens, rank)
    wide = jax.ShapeDtypeStruct((tokens, per_dev * group), BF)
    narrow = jax.ShapeDtypeStruct((tokens, per_dev * width), BF)
    tile_shape = jax.ShapeDtypeStruct(bfly.shape, F32)
    v_shape = jax.ShapeDtypeStruct(lr_v.shape, F32)

    def to_partner(block, section):
        return crossed(block, "feat", 1 << (section - local_bits))

    env = {}

    def pin(value, *names):
        names = [n for n in names if n in env]
        if names:
            value, *rest = tie(value, *[env[n] for n in names])
            env.update(zip(names, rest))
        return value

    def each(prefix, *tails):
        return [f"{prefix}{d}{t}" for d in others for t in tails or ("",)]

    far = remote[-1:]
    near = remote[:-1]
    lead = 1
    parts = [(0, lead), (lead, per_dev)] if per_dev > lead else [(0, lead)]

    low_part = jnp.dot(inputs, lr_u, preferred_element_type=F32)
    for s in reversed(near[2:] + far):
        env[f"x{s}"] = to_partner(inputs, s)
    for s in near[1:2]:
        env[f"x{s}"] = to_partner(tie(inputs, low_part)[0], s)
    joined = jnp.concatenate([cotangent[:, : lead * group], inputs], axis=1)
    for d in others:
        env[f"in{d}"] = rolled(joined, "dp", d)

    def cut_rest():
        pieces = [cotangent[:, lead * group :]] if per_dev > lead else []
        pieces += [env[f"x{s}"] for s in far]
        env["cut"] = jnp.concatenate(pieces, axis=1) if len(pieces) > 1 else pieces[0]

    def send_rest(value):
        piece = tie(env["cut"], value)[0]
        for d in others:
            env[f"rest{d}"] = rolled(piece, "dp", d)

    def low_hooks(step, value):
        if step == "scatter1":
            value = pin(value, *[f"x{s}" for s in near[1:] + far])
            cut_rest()
        if step == "far":
            value = pin(value, *each("in"), "cut")
        return value

    low = sum_far(scatter_near(low_part, "feat", low_hooks, False), "feat", low_hooks)
    for s in near[:1]:
        env[f"x{s}"] = to_partner(tie(inputs, low)[0], s)
    for d in others:
        env[f"low{d}"] = rolled(low, "dp", d)
    low = gather_near(low, "feat", False)
    for d in others:
        env[f"cot{d}0"] = env[f"in{d}"]
        env[f"in{d}"] = env[f"in{d}"][:, lead * group :]
        for s in near[1:]:
            env[f"xo{d}{s}"] = to_partner(tie(env[f"in{d}"], low)[0], s)
    send_rest(env["low1"] if others else low)
    low = pin(low, *[f"x{s}" for s in remote])

    def x_blocks(base_block, prefix):
        arrays = [env.get(f"{prefix}{s}", base_block) for s in range(sections)]
        return arrays, [column(tokens, width, flip) for flip in flips]

    arrays, specs = x_blocks(inputs, "x")
    term_specs = [column(tokens, width, flip) for flip in flips]
    out = call(
        functools.partial(forward_kernel, [1] * sections),
        per_dev,
        specs + [tile_spec(), low_spec, row(rank, group), row(tokens, group)],
        [row(tokens, group), row(tokens, group), resident(tokens, rank)] + term_specs,
        [pltpu.HBM(wide.shape, BF)] * 2
        + [pltpu.HBM((tokens, rank), F32)]
        + [pltpu.HBM(narrow.shape, BF)] * sections,
        (1000, 1000),
        name="forward",
    )(*[a if s in near[:1] else in_hbm(a) for s, a in enumerate(arrays)], in_hbm(bfly), low, lr_v, in_hbm(cotangent))
    activated, d_pre, d_low_part = out[:3]
    terms = list(out[3:])
    for d in others:
        env[f"low{d}"] = gather_near(tie(env[f"low{d}"], d_low_part)[0], "feat", False)

    def send_terms(value, which):
        for s in reversed(which):
            env[f"t{s}"] = to_partner(tie(terms[s], value)[0], s)

    def d_low_hooks(step, value):
        if step == "scatter":
            for d in others:
                for s in near[:1]:
                    env[f"xo{d}{s}"] = to_partner(tie(env[f"in{d}"], value)[0], s)
        if step == "far":
            send_terms(value, near[1:] + far)
        return value

    d_low_part = pin(d_low_part, *each("xo", *near[1:]))
    d_low = sum_far(scatter_near(d_low_part, "feat", d_low_hooks, True), "feat", d_low_hooks)
    d_low = gather_near(pin(d_low, *each("low")), "feat", True)
    for d in others:
        env[f"d_low{d}"] = rolled(d_low, "dp", d)

    grads = []
    for d in [0, *others] if data_groups == 1 or data_groups > 2 else [1]:
        own, other = d == 0 or data_groups == 2, d > 0
        last = scale if d == data_groups - 1 else 1.0
        operands, blocks = [], []
        if own:
            operands += arrays + [low, d_pre]
            blocks += specs + [low_spec, row(tokens, group)]
        if other:
            x_others, x_specs = x_blocks(env[f"in{d}"], f"xo{d}")
            for s in far:
                x_others[s] = env[f"rest{d}"]
                x_specs[s] = column(tokens, width, 0, (per_dev - lead) * group // width)
            cots = [in_hbm(a) for a in (env[f"cot{d}0"], env[f"rest{d}"])[: len(parts)]]
            operands += x_others + [in_hbm(bfly), env[f"low{d}"], lr_v] + cots
            blocks += x_specs + [tile_spec(), low_spec, row(rank, group)]
            blocks += [clipped(tokens, group, p[0], p[1] - p[0]) for p in parts]
        count = len(operands)
        grads = call(
            functools.partial(
                weight_grad_kernel, sections, own, other, [p[0] for p in parts], last
            ),
            per_dev,
            blocks + ([tile_spec(), row(rank, group)] if grads else []),
            [tile_spec(), row(rank, group)],
            [tile_shape, v_shape],
            (1000, 1000),
            aliases={count: 0, count + 1: 1} if grads else None,
            name="weight_grad",
        )(*map(in_hbm, operands), *grads)
    d_bfly, d_v = grads

    send_terms(d_low, [s for s in remote if f"t{s}" not in env])
    d_low, d_v = tie(d_low, d_v)
    last_arrays = [env.get(f"t{s}", terms[s]) for s in range(sections)] + [d_low, lr_u, inputs]
    for d in others:
        last_arrays += [env[f"in{d}"], env[f"d_low{d}"]]
    d_inputs, d_u = call(
        functools.partial(finish_kernel, sections, data_groups - 1, scale),
        1,
        [resident(*a.shape) for a in last_arrays],
        [resident(*narrow.shape), resident(*lr_u.shape)],
        [narrow, jax.ShapeDtypeStruct(lr_u.shape, F32)],
        (1000, 1000),
        name="finish",
    )(*last_arrays)
    return activated, d_inputs, d_bfly, d_u, d_v


def solution(mesh):
    return jax.shard_map(
        local,
        mesh=mesh,
        in_specs=(
            P("dp", "feat"),
            P("feat", None, None, None),
            P("feat", None),
            P(None, "feat"),
            P("dp", "feat"),
        ),
        out_specs=(
            P("dp", "feat"),
            P("dp", "feat"),
            P("feat", None, None, None),
            P("feat", None),
            P(None, "feat"),
        ),
        check_vma=False,
    )
```

```python
import functools

import jax
import jax.numpy as jnp
import numpy as np
from jax import lax
from jax.experimental import pallas as pl
from jax.experimental.pallas import tpu as pltpu
from jax.sharding import PartitionSpec as P

BF = jnp.bfloat16
F32 = jnp.float32
VMEM_LIMIT = 32 * 1024 * 1024
GELU_C = float(np.sqrt(2.0 / np.pi))
GELU_A = 0.044715


def crossed(block, axis, mask):
    count = lax.axis_size(axis)
    return lax.ppermute(block, axis, [(i, i ^ mask) for i in range(count)])


def rolled(block, axis, shift):
    count = lax.axis_size(axis)
    return lax.ppermute(block, axis, [(i, (i + shift) % count) for i in range(count)])


def scatter_half(part, bit, axis):
    rows = part.shape[0] // 2
    mine = (lax.axis_index(axis) >> bit) & 1
    keep = lax.dynamic_slice_in_dim(part, mine * rows, rows, 0)
    send = lax.dynamic_slice_in_dim(part, (1 - mine) * rows, rows, 0)
    return keep + crossed(send.astype(BF), axis, 1 << bit).astype(F32)


def tie(value, *others):
    return lax.optimization_barrier((value, *others))


def no_hooks(step, value):
    return value


def near_bits(axis):
    return min(lax.axis_size(axis).bit_length() - 1, 2)


def scatter_near(part, axis, hooks, direct):
    near = near_bits(axis)
    if not direct:
        for bit in range(near):
            part = hooks(f"scatter{bit}", scatter_half(part, bit, axis))
        return part
    count = 1 << near
    rows = part.shape[0] // count
    mine = lax.axis_index(axis) & (count - 1)
    total = lax.dynamic_slice_in_dim(part, mine * rows, rows, 0)
    for mask in range(1, count):
        send = lax.dynamic_slice_in_dim(part, (mine ^ mask) * rows, rows, 0)
        total = total + crossed(send.astype(BF), axis, mask).astype(F32)
    return hooks("scatter", total)


def sum_far(part, axis, hooks):
    near = near_bits(axis)
    sent = part.astype(BF)
    for mask in reversed(range(1, lax.axis_size(axis) >> near)):
        part = part + crossed(sent, axis, mask << near).astype(F32)
    return hooks("far", part).astype(BF)


def gather_near(part, axis, direct):
    near = near_bits(axis)
    mine = lax.axis_index(axis)
    held = [part] + [crossed(part, axis, mask) for mask in range(1, 1 << near)]
    for bit in range(near):
        swap = (mine >> bit) & 1
        held = [jnp.where(swap == 0, h, held[i ^ (1 << bit)]) for i, h in enumerate(held)]
    if not direct and near == 2:
        held = [held[i] for i in (0, 2, 1, 3)]
    return jnp.concatenate(held, 0)


def gelu_parts(pre):
    square = pre * pre
    tanh = jnp.tanh(GELU_C * (pre + GELU_A * (square * pre)))
    half = 0.5 * (1.0 + tanh)
    slope = half + (0.5 * GELU_C) * pre * (1.0 - tanh * tanh) * (1.0 + (3.0 * GELU_A) * square)
    return pre * half, slope


def nt(a, b):
    return lax.dot_general(a, b, (((1,), (1,)), ((), ())), preferred_element_type=F32)


def tn(a, b):
    return lax.dot_general(a, b, (((0,), (0,)), ((), ())), preferred_element_type=F32)


def gathered(refs, pieces):
    refs = iter(refs)
    columns = []
    for count in pieces:
        rows = [next(refs)[...] for _ in range(count)]
        columns.append(rows[0] if count == 1 else jnp.concatenate(rows, axis=0))
    return columns[0] if len(columns) == 1 else jnp.concatenate(columns, axis=1)


def forward_kernel(pieces, *refs):
    sections, count = len(pieces), sum(pieces)
    x = refs[:count]
    bfly, low, lr_v, cot, act, d_pre, d_low = refs[count : count + 7]
    terms = refs[count + 7 :]
    width = bfly.shape[2]
    tiles = bfly[0].reshape(sections * width, bfly.shape[3])
    block = gathered(x, pieces)
    pre = jnp.dot(block, tiles, preferred_element_type=F32) + jnp.dot(
        low[...], lr_v[...], preferred_element_type=F32
    )
    value, slope = gelu_parts(pre)
    act[...] = value.astype(BF)
    grad = (cot[...].astype(F32) * slope).astype(BF)
    d_pre[...] = grad
    part = nt(grad, lr_v[...])

    @pl.when(pl.program_id(0) == 0)
    def _():
        d_low[...] = part

    @pl.when(pl.program_id(0) > 0)
    def _():
        d_low[...] += part

    back = nt(grad, tiles).astype(BF)
    for section in range(sections):
        terms[section][...] = back[:, section * width : (section + 1) * width]


def weight_grad_kernel(sections, own, other, starts, scale, *refs):
    refs = list(refs)

    def take(count):
        taken, refs[:] = refs[:count], refs[count:]
        return taken

    def side(x):
        return jnp.concatenate([ref[...] for ref in x], axis=1)

    blocks, lows, grads = [], [], []
    if own:
        blocks.append(side(take(sections)))
        low, grad = take(2)
        lows.append(low[...])
        grads.append(grad[...])
    if other:
        block = side(take(sections))
        bfly, low, lr_v = take(3)
        cots = take(len(starts))
        cot = cots[0][...]
        for start, piece in zip(starts[1:], cots[1:]):
            cot = jnp.where(pl.program_id(0) >= start, piece[...], cot)
        tiles = bfly[0].reshape(sections * bfly.shape[2], bfly.shape[3])
        pre = jnp.dot(block, tiles, preferred_element_type=F32) + jnp.dot(
            low[...], lr_v[...], preferred_element_type=F32
        )
        _, slope = gelu_parts(pre)
        blocks.append(block)
        lows.append(low[...])
        grads.append((cot.astype(F32) * slope).astype(BF))
    block, low, grad = (
        a[0] if len(a) == 1 else jnp.concatenate(a, axis=0) for a in (blocks, lows, grads)
    )
    total, total_v = tn(block, grad), tn(low, grad)
    if not own:
        d_bfly_in, d_v_in = take(2)
        total = total + d_bfly_in[0].reshape(total.shape)
        total_v = total_v + d_v_in[...]
    d_bfly, d_v = refs
    d_bfly[0] = (total * scale).reshape(d_bfly.shape[1:])
    d_v[...] = total_v * scale


def finish_kernel(sections, others, scale, *refs):
    terms, (d_low, lr_u, x), rest = refs[:sections], refs[sections : sections + 3], refs[sections + 3 :]
    d_inputs, d_u = rest[2 * others :]
    total = nt(d_low[...], lr_u[...])
    for term in terms:
        total = total + term[...].astype(F32)
    d_inputs[...] = total.astype(BF)
    grad = tn(x[...], d_low[...])
    for other in range(others):
        grad = grad + tn(rest[2 * other][...], rest[2 * other + 1][...])
    d_u[...] = grad * scale


def column(rows, width, flip, base=0, at=0):
    return pl.BlockSpec((rows, width), lambda g: (at, (g + base) ^ flip))


def row(rows, width, base=0, at=0):
    return pl.BlockSpec((rows, width), lambda g: (at, g + base))


def clipped(rows, width, start, count):
    return pl.BlockSpec((rows, width), lambda g: (0, jnp.clip(g - start, 0, count - 1)))


def in_hbm(array):
    return pltpu.with_memory_space_constraint(array, pltpu.HBM)


def resident(*shape):
    return pl.BlockSpec(shape, lambda g: (0,) * len(shape))


def call(kernel, grid, in_specs, out_specs, out_shape, cost, aliases=None, name=None):
    return pl.pallas_call(
        kernel,
        grid=(grid,),
        in_specs=in_specs,
        out_specs=out_specs,
        out_shape=out_shape,
        input_output_aliases=aliases or {},
        cost_estimate=pl.CostEstimate(flops=cost[0], bytes_accessed=cost[1], transcendentals=0),
        compiler_params=pltpu.CompilerParams(vmem_limit_bytes=VMEM_LIMIT),
        name=name,
    )


def local(inputs, bfly, lr_u, lr_v, cotangent):
    tokens = inputs.shape[0]
    per_dev, sections, width, group = bfly.shape
    levels = sections - 1
    rank = lr_v.shape[0]
    local_bits = per_dev.bit_length() - 1
    data_groups = lax.axis_size("dp")
    scale = float(1.0 / np.sqrt(np.float32(tokens * data_groups)))
    remote = list(range(local_bits, levels))
    others = range(1, data_groups)

    flips = [(1 << s) if s < local_bits else 0 for s in range(sections)]

    def tile_spec(base=0):
        return pl.BlockSpec((1, sections, width, group), lambda g: (g + base, 0, 0, 0))

    low_spec = resident(tokens, rank)
    wide = jax.ShapeDtypeStruct((tokens, per_dev * group), BF)
    narrow = jax.ShapeDtypeStruct((tokens, per_dev * width), BF)
    tile_shape = jax.ShapeDtypeStruct(bfly.shape, F32)
    v_shape = jax.ShapeDtypeStruct(lr_v.shape, F32)

    def to_partner(block, section):
        return crossed(block, "feat", 1 << (section - local_bits))

    env = {}

    def pin(value, *names):
        names = [n for n in names if n in env]
        if names:
            value, *rest = tie(value, *[env[n] for n in names])
            env.update(zip(names, rest))
        return value

    def each(prefix, *tails):
        return [f"{prefix}{d}{t}" for d in others for t in tails or ("",)]

    far = remote[-1:]
    near = remote[:-1]
    lead = 1
    parts = [(0, lead), (lead, per_dev)] if per_dev > lead else [(0, lead)]

    low_part = jnp.dot(inputs, lr_u, preferred_element_type=F32)
    for s in reversed(near[2:] + far):
        env[f"x{s}"] = to_partner(inputs, s)
    for s in near[1:2]:
        env[f"x{s}"] = to_partner(tie(inputs, low_part)[0], s)
    joined = jnp.concatenate([cotangent[:, : lead * group], inputs], axis=1)
    for d in others:
        env[f"in{d}"] = rolled(joined, "dp", d)

    def cut_rest():
        pieces = [cotangent[:, lead * group :]] if per_dev > lead else []
        pieces += [env[f"x{s}"] for s in far]
        env["cut"] = jnp.concatenate(pieces, axis=1) if len(pieces) > 1 else pieces[0]

    def send_rest(value):
        piece = tie(env["cut"], value)[0]
        for d in others:
            env[f"rest{d}"] = rolled(piece, "dp", d)

    def low_hooks(step, value):
        if step == "scatter1":
            value = pin(value, *[f"x{s}" for s in near[1:] + far])
            cut_rest()
        if step == "far":
            value = pin(value, *each("in"), "cut")
        return value

    low = sum_far(scatter_near(low_part, "feat", low_hooks, False), "feat", low_hooks)
    for s in near[:1]:
        env[f"x{s}"] = to_partner(tie(inputs, low)[0], s)
    for d in others:
        env[f"low{d}"] = rolled(low, "dp", d)
    low = gather_near(low, "feat", False)
    for d in others:
        env[f"cot{d}0"] = env[f"in{d}"]
        env[f"in{d}"] = env[f"in{d}"][:, lead * group :]
        for s in near[1:]:
            env[f"xo{d}{s}"] = to_partner(tie(env[f"in{d}"], low)[0], s)
    send_rest(env["low1"] if others else low)
    low = pin(low, *[f"x{s}" for s in remote], *each("low"))

    def x_blocks(base_block, prefix):
        arrays = [env.get(f"{prefix}{s}", base_block) for s in range(sections)]
        return arrays, [column(tokens, width, flip) for flip in flips]

    arrays, specs = x_blocks(inputs, "x")
    term_specs = [column(tokens, width, flip) for flip in flips]
    out = call(
        functools.partial(forward_kernel, [1] * sections),
        per_dev,
        specs + [tile_spec(), low_spec, row(rank, group), row(tokens, group)],
        [row(tokens, group), row(tokens, group), resident(tokens, rank)] + term_specs,
        [pltpu.HBM(wide.shape, BF)] * 2
        + [pltpu.HBM((tokens, rank), F32)]
        + [pltpu.HBM(narrow.shape, BF)] * sections,
        (1000, 1000),
        name="forward",
    )(*[a if s in near[:1] else in_hbm(a) for s, a in enumerate(arrays)], in_hbm(bfly), low, lr_v, in_hbm(cotangent))
    activated, d_pre, d_low_part = out[:3]
    terms = list(out[3:])
    for d in others:
        env[f"low{d}"] = gather_near(tie(env[f"low{d}"], d_low_part)[0], "feat", False)

    def send_terms(value, which):
        for s in reversed(which):
            env[f"t{s}"] = to_partner(tie(terms[s], value)[0], s)

    def d_low_hooks(step, value):
        if step == "scatter":
            for d in others:
                for s in near[:1]:
                    env[f"xo{d}{s}"] = to_partner(tie(env[f"in{d}"], value)[0], s)
        if step == "far":
            send_terms(value, near[1:] + far)
        return value

    d_low_part = pin(d_low_part, *each("xo", *near[1:]))
    d_low = sum_far(scatter_near(d_low_part, "feat", d_low_hooks, True), "feat", d_low_hooks)
    d_low = gather_near(pin(d_low, *each("low")), "feat", True)
    for d in others:
        env[f"d_low{d}"] = rolled(d_low, "dp", d)

    grads = []
    for d in [0, *others] if data_groups == 1 or data_groups > 2 else [1]:
        own, other = d == 0 or data_groups == 2, d > 0
        last = scale if d == data_groups - 1 else 1.0
        operands, blocks = [], []
        if own:
            operands += arrays + [low, d_pre]
            blocks += specs + [low_spec, row(tokens, group)]
        if other:
            x_others, x_specs = x_blocks(env[f"in{d}"], f"xo{d}")
            for s in far:
                x_others[s] = env[f"rest{d}"]
                x_specs[s] = column(tokens, width, 0, (per_dev - lead) * group // width)
            cots = [in_hbm(a) for a in (env[f"cot{d}0"], env[f"rest{d}"])[: len(parts)]]
            operands += x_others + [in_hbm(bfly), env[f"low{d}"], lr_v] + cots
            blocks += x_specs + [tile_spec(), low_spec, row(rank, group)]
            blocks += [clipped(tokens, group, p[0], p[1] - p[0]) for p in parts]
        count = len(operands)
        grads = call(
            functools.partial(
                weight_grad_kernel, sections, own, other, [p[0] for p in parts], last
            ),
            per_dev,
            blocks + ([tile_spec(), row(rank, group)] if grads else []),
            [tile_spec(), row(rank, group)],
            [tile_shape, v_shape],
            (1000, 1000),
            aliases={count: 0, count + 1: 1} if grads else None,
            name="weight_grad",
        )(*operands, *grads)
    d_bfly, d_v = grads

    send_terms(d_low, [s for s in remote if f"t{s}" not in env])
    d_low, d_v = tie(d_low, d_v)
    last_arrays = [env.get(f"t{s}", terms[s]) for s in range(sections)] + [d_low, lr_u, inputs]
    for d in others:
        last_arrays += [env[f"in{d}"], env[f"d_low{d}"]]
    d_inputs, d_u = call(
        functools.partial(finish_kernel, sections, data_groups - 1, scale),
        1,
        [resident(*a.shape) for a in last_arrays],
        [resident(*narrow.shape), resident(*lr_u.shape)],
        [narrow, jax.ShapeDtypeStruct(lr_u.shape, F32)],
        (1000, 1000),
        name="finish",
    )(*last_arrays)
    return activated, d_inputs, d_bfly, d_u, d_v


def solution(mesh):
    return jax.shard_map(
        local,
        mesh=mesh,
        in_specs=(
            P("dp", "feat"),
            P("feat", None, None, None),
            P("feat", None),
            P(None, "feat"),
            P("dp", "feat"),
        ),
        out_specs=(
            P("dp", "feat"),
            P("dp", "feat"),
            P("feat", None, None, None),
            P("feat", None),
            P(None, "feat"),
        ),
        check_vma=False,
    )
```

```python
import functools

import jax
import jax.numpy as jnp
import numpy as np
from jax import lax
from jax.experimental import pallas as pl
from jax.experimental.pallas import tpu as pltpu
from jax.sharding import PartitionSpec as P

BF = jnp.bfloat16
F32 = jnp.float32
VMEM_LIMIT = 32 * 1024 * 1024
GELU_C = float(np.sqrt(2.0 / np.pi))
GELU_A = 0.044715


def crossed(block, axis, mask):
    count = lax.axis_size(axis)
    return lax.ppermute(block, axis, [(i, i ^ mask) for i in range(count)])


def rolled(block, axis, shift):
    count = lax.axis_size(axis)
    return lax.ppermute(block, axis, [(i, (i + shift) % count) for i in range(count)])


def scatter_half(part, bit, axis):
    rows = part.shape[0] // 2
    mine = (lax.axis_index(axis) >> bit) & 1
    keep = lax.dynamic_slice_in_dim(part, mine * rows, rows, 0)
    send = lax.dynamic_slice_in_dim(part, (1 - mine) * rows, rows, 0)
    return keep + crossed(send.astype(BF), axis, 1 << bit).astype(F32)


def tie(value, *others):
    return lax.optimization_barrier((value, *others))


def no_hooks(step, value):
    return value


def near_bits(axis):
    return min(lax.axis_size(axis).bit_length() - 1, 2)


def scatter_near(part, axis, hooks, direct):
    near = near_bits(axis)
    if not direct:
        for bit in range(near):
            part = hooks(f"scatter{bit}", scatter_half(part, bit, axis))
        return part
    count = 1 << near
    rows = part.shape[0] // count
    mine = lax.axis_index(axis) & (count - 1)
    total = lax.dynamic_slice_in_dim(part, mine * rows, rows, 0)
    for mask in range(1, count):
        send = lax.dynamic_slice_in_dim(part, (mine ^ mask) * rows, rows, 0)
        total = total + crossed(send.astype(BF), axis, mask).astype(F32)
    return hooks("scatter", total)


def sum_far(part, axis, hooks):
    near = near_bits(axis)
    sent = part.astype(BF)
    for mask in reversed(range(1, lax.axis_size(axis) >> near)):
        part = part + crossed(sent, axis, mask << near).astype(F32)
    return hooks("far", part).astype(BF)


def gather_near(part, axis, direct):
    near = near_bits(axis)
    mine = lax.axis_index(axis)
    held = [part] + [crossed(part, axis, mask) for mask in range(1, 1 << near)]
    for bit in range(near):
        swap = (mine >> bit) & 1
        held = [jnp.where(swap == 0, h, held[i ^ (1 << bit)]) for i, h in enumerate(held)]
    if not direct and near == 2:
        held = [held[i] for i in (0, 2, 1, 3)]
    return jnp.concatenate(held, 0)


def gelu_parts(pre):
    square = pre * pre
    tanh = jnp.tanh(GELU_C * (pre + GELU_A * (square * pre)))
    half = 0.5 * (1.0 + tanh)
    slope = half + (0.5 * GELU_C) * pre * (1.0 - tanh * tanh) * (1.0 + (3.0 * GELU_A) * square)
    return pre * half, slope


def nt(a, b):
    return lax.dot_general(a, b, (((1,), (1,)), ((), ())), preferred_element_type=F32)


def tn(a, b):
    return lax.dot_general(a, b, (((0,), (0,)), ((), ())), preferred_element_type=F32)


def gathered(refs, pieces):
    refs = iter(refs)
    columns = []
    for count in pieces:
        rows = [next(refs)[...] for _ in range(count)]
        columns.append(rows[0] if count == 1 else jnp.concatenate(rows, axis=0))
    return columns[0] if len(columns) == 1 else jnp.concatenate(columns, axis=1)


def forward_kernel(pieces, *refs):
    sections, count = len(pieces), sum(pieces)
    x = refs[:count]
    bfly, low, lr_v, cot, act, d_pre, d_low = refs[count : count + 7]
    terms = refs[count + 7 :]
    width = bfly.shape[2]
    tiles = bfly[0].reshape(sections * width, bfly.shape[3])
    block = gathered(x, pieces)
    pre = jnp.dot(block, tiles, preferred_element_type=F32) + jnp.dot(
        low[...], lr_v[...], preferred_element_type=F32
    )
    value, slope = gelu_parts(pre)
    act[...] = value.astype(BF)
    grad = (cot[...].astype(F32) * slope).astype(BF)
    d_pre[...] = grad
    part = nt(grad, lr_v[...])

    @pl.when(pl.program_id(0) == 0)
    def _():
        d_low[...] = part

    @pl.when(pl.program_id(0) > 0)
    def _():
        d_low[...] += part

    back = nt(grad, tiles).astype(BF)
    for section in range(sections):
        terms[section][...] = back[:, section * width : (section + 1) * width]


def weight_grad_kernel(sections, own, other, starts, scale, *refs):
    refs = list(refs)

    def take(count):
        taken, refs[:] = refs[:count], refs[count:]
        return taken

    def side(x):
        return jnp.concatenate([ref[...] for ref in x], axis=1)

    blocks, lows, grads = [], [], []
    if own:
        blocks.append(side(take(sections)))
        low, grad = take(2)
        lows.append(low[...])
        grads.append(grad[...])
    if other:
        block = side(take(sections))
        bfly, low, lr_v = take(3)
        cots = take(len(starts))
        cot = cots[0][...]
        for start, piece in zip(starts[1:], cots[1:]):
            cot = jnp.where(pl.program_id(0) >= start, piece[...], cot)
        tiles = bfly[0].reshape(sections * bfly.shape[2], bfly.shape[3])
        pre = jnp.dot(block, tiles, preferred_element_type=F32) + jnp.dot(
            low[...], lr_v[...], preferred_element_type=F32
        )
        _, slope = gelu_parts(pre)
        blocks.append(block)
        lows.append(low[...])
        grads.append((cot.astype(F32) * slope).astype(BF))
    block, low, grad = (
        a[0] if len(a) == 1 else jnp.concatenate(a, axis=0) for a in (blocks, lows, grads)
    )
    total, total_v = tn(block, grad), tn(low, grad)
    if not own:
        d_bfly_in, d_v_in = take(2)
        total = total + d_bfly_in[0].reshape(total.shape)
        total_v = total_v + d_v_in[...]
    d_bfly, d_v = refs
    d_bfly[0] = (total * scale).reshape(d_bfly.shape[1:])
    d_v[...] = total_v * scale


def finish_kernel(sections, others, scale, *refs):
    terms, (d_low, lr_u, x), rest = refs[:sections], refs[sections : sections + 3], refs[sections + 3 :]
    d_inputs, d_u = rest[2 * others :]
    total = nt(d_low[...], lr_u[...])
    for term in terms:
        total = total + term[...].astype(F32)
    d_inputs[...] = total.astype(BF)
    grad = tn(x[...], d_low[...])
    for other in range(others):
        grad = grad + tn(rest[2 * other][...], rest[2 * other + 1][...])
    grad = grad * scale

    @pl.when(pl.program_id(0) == 0)
    def _():
        d_u[...] = grad

    @pl.when(pl.program_id(0) > 0)
    def _():
        d_u[...] += grad


def column(rows, width, flip, base=0, at=0):
    return pl.BlockSpec((rows, width), lambda g: (at, (g + base) ^ flip))


def row(rows, width, base=0, at=0):
    return pl.BlockSpec((rows, width), lambda g: (at, g + base))


def clipped(rows, width, start, count):
    return pl.BlockSpec((rows, width), lambda g: (0, jnp.clip(g - start, 0, count - 1)))


def in_hbm(array):
    return pltpu.with_memory_space_constraint(array, pltpu.HBM)


def resident(*shape):
    return pl.BlockSpec(shape, lambda g: (0,) * len(shape))


def call(kernel, grid, in_specs, out_specs, out_shape, cost, aliases=None, name=None):
    return pl.pallas_call(
        kernel,
        grid=(grid,),
        in_specs=in_specs,
        out_specs=out_specs,
        out_shape=out_shape,
        input_output_aliases=aliases or {},
        cost_estimate=pl.CostEstimate(flops=cost[0], bytes_accessed=cost[1], transcendentals=0),
        compiler_params=pltpu.CompilerParams(vmem_limit_bytes=VMEM_LIMIT),
        name=name,
    )


def local(inputs, bfly, lr_u, lr_v, cotangent):
    tokens = inputs.shape[0]
    per_dev, sections, width, group = bfly.shape
    levels = sections - 1
    rank = lr_v.shape[0]
    local_bits = per_dev.bit_length() - 1
    data_groups = lax.axis_size("dp")
    scale = float(1.0 / np.sqrt(np.float32(tokens * data_groups)))
    remote = list(range(local_bits, levels))
    others = range(1, data_groups)

    flips = [(1 << s) if s < local_bits else 0 for s in range(sections)]

    def tile_spec(base=0):
        return pl.BlockSpec((1, sections, width, group), lambda g: (g + base, 0, 0, 0))

    low_spec = resident(tokens, rank)
    wide = jax.ShapeDtypeStruct((tokens, per_dev * group), BF)
    narrow = jax.ShapeDtypeStruct((tokens, per_dev * width), BF)
    tile_shape = jax.ShapeDtypeStruct(bfly.shape, F32)
    v_shape = jax.ShapeDtypeStruct(lr_v.shape, F32)

    def to_partner(block, section):
        return crossed(block, "feat", 1 << (section - local_bits))

    env = {}

    def pin(value, *names):
        names = [n for n in names if n in env]
        if names:
            value, *rest = tie(value, *[env[n] for n in names])
            env.update(zip(names, rest))
        return value

    def each(prefix, *tails):
        return [f"{prefix}{d}{t}" for d in others for t in tails or ("",)]

    far = remote[-1:]
    near = remote[:-1]
    lead = 1
    parts = [(0, lead), (lead, per_dev)] if per_dev > lead else [(0, lead)]

    low_part = jnp.dot(inputs, lr_u, preferred_element_type=F32)
    for s in reversed(near[2:] + far):
        env[f"x{s}"] = to_partner(inputs, s)
    for s in near[1:2]:
        env[f"x{s}"] = to_partner(tie(inputs, low_part)[0], s)
    joined = jnp.concatenate([cotangent[:, : lead * group], inputs], axis=1)
    for d in others:
        env[f"in{d}"] = rolled(joined, "dp", d)

    def cut_rest():
        pieces = [cotangent[:, lead * group :]] if per_dev > lead else []
        pieces += [env[f"x{s}"] for s in far]
        env["cut"] = jnp.concatenate(pieces, axis=1) if len(pieces) > 1 else pieces[0]

    def send_rest(value):
        piece = tie(env["cut"], value)[0]
        for d in others:
            env[f"rest{d}"] = rolled(piece, "dp", d)

    def low_hooks(step, value):
        if step == "scatter1":
            value = pin(value, *[f"x{s}" for s in near[1:] + far])
            cut_rest()
        if step == "far":
            value = pin(value, *each("in"), "cut")
        return value

    low = sum_far(scatter_near(low_part, "feat", low_hooks, False), "feat", low_hooks)
    for s in near[:1]:
        env[f"x{s}"] = to_partner(tie(inputs, low)[0], s)
    for d in others:
        env[f"low{d}"] = rolled(low, "dp", d)
    low = gather_near(low, "feat", False)
    for d in others:
        env[f"cot{d}0"] = env[f"in{d}"]
        env[f"in{d}"] = env[f"in{d}"][:, lead * group :]
        for s in near[1:]:
            env[f"xo{d}{s}"] = to_partner(tie(env[f"in{d}"], low)[0], s)
    send_rest(env["low1"] if others else low)
    low = pin(low, *[f"x{s}" for s in remote], *each("low"))

    def x_blocks(base_block, prefix):
        arrays = [env.get(f"{prefix}{s}", base_block) for s in range(sections)]
        return arrays, [column(tokens, width, flip) for flip in flips]

    arrays, specs = x_blocks(inputs, "x")
    term_specs = [column(tokens, width, flip) for flip in flips]
    out = call(
        functools.partial(forward_kernel, [1] * sections),
        per_dev,
        specs + [tile_spec(), low_spec, row(rank, group), row(tokens, group)],
        [row(tokens, group), row(tokens, group), resident(tokens, rank)] + term_specs,
        [pltpu.HBM(wide.shape, BF)] * 2
        + [pltpu.HBM((tokens, rank), F32)]
        + [pltpu.HBM(narrow.shape, BF)] * sections,
        (1000, 1000),
        name="forward",
    )(*[a if s in near[:1] else in_hbm(a) for s, a in enumerate(arrays)], in_hbm(bfly), low, lr_v, in_hbm(cotangent))
    activated, d_pre, d_low_part = out[:3]
    terms = list(out[3:])
    for d in others:
        env[f"low{d}"] = gather_near(tie(env[f"low{d}"], d_low_part)[0], "feat", False)

    def send_terms(value, which):
        for s in reversed(which):
            env[f"t{s}"] = to_partner(tie(terms[s], value)[0], s)

    def d_low_hooks(step, value):
        if step == "scatter":
            for d in others:
                for s in near[:1]:
                    env[f"xo{d}{s}"] = to_partner(tie(env[f"in{d}"], value)[0], s)
        if step == "far":
            send_terms(value, near[1:] + far)
        return value

    d_low_part = pin(d_low_part, *each("xo", *near[1:]))
    d_low = sum_far(scatter_near(d_low_part, "feat", d_low_hooks, True), "feat", d_low_hooks)
    d_low = gather_near(pin(d_low, *each("low")), "feat", True)
    for d in others:
        env[f"d_low{d}"] = rolled(d_low, "dp", d)

    grads = []
    for d in [0, *others] if data_groups == 1 or data_groups > 2 else [1]:
        own, other = d == 0 or data_groups == 2, d > 0
        last = scale if d == data_groups - 1 else 1.0
        operands, blocks = [], []
        if own:
            operands += arrays + [low, d_pre]
            blocks += specs + [low_spec, row(tokens, group)]
        if other:
            x_others, x_specs = x_blocks(env[f"in{d}"], f"xo{d}")
            for s in far:
                x_others[s] = env[f"rest{d}"]
                x_specs[s] = column(tokens, width, 0, (per_dev - lead) * group // width)
            cots = [in_hbm(a) for a in (env[f"cot{d}0"], env[f"rest{d}"])[: len(parts)]]
            operands += x_others + [in_hbm(bfly), env[f"low{d}"], lr_v] + cots
            blocks += x_specs + [tile_spec(), low_spec, row(rank, group)]
            blocks += [clipped(tokens, group, p[0], p[1] - p[0]) for p in parts]
        count = len(operands)
        grads = call(
            functools.partial(
                weight_grad_kernel, sections, own, other, [p[0] for p in parts], last
            ),
            per_dev,
            blocks + ([tile_spec(), row(rank, group)] if grads else []),
            [tile_spec(), row(rank, group)],
            [tile_shape, v_shape],
            (1000, 1000),
            aliases={count: 0, count + 1: 1} if grads else None,
            name="weight_grad",
        )(*operands, *grads)
    d_bfly, d_v = grads

    send_terms(d_low, [s for s in remote if f"t{s}" not in env])
    d_low, d_v = tie(d_low, d_v)
    last_arrays = [env.get(f"t{s}", terms[s]) for s in range(sections)] + [d_low, lr_u, inputs]
    for d in others:
        last_arrays += [env[f"in{d}"], env[f"d_low{d}"]]

    def rows_of(columns):
        return pl.BlockSpec((tokens // 2, columns), lambda i: (i, 0))

    d_inputs, d_u = call(
        functools.partial(finish_kernel, sections, data_groups - 1, scale),
        2,
        [resident(*a.shape) if a is lr_u else rows_of(a.shape[1]) for a in last_arrays],
        [rows_of(per_dev * width), resident(*lr_u.shape)],
        [narrow, jax.ShapeDtypeStruct(lr_u.shape, F32)],
        (1000, 1000),
        name="finish",
    )(*last_arrays)
    return activated, d_inputs, d_bfly, d_u, d_v


def solution(mesh):
    return jax.shard_map(
        local,
        mesh=mesh,
        in_specs=(
            P("dp", "feat"),
            P("feat", None, None, None),
            P("feat", None),
            P(None, "feat"),
            P("dp", "feat"),
        ),
        out_specs=(
            P("dp", "feat"),
            P("dp", "feat"),
            P("feat", None, None, None),
            P("feat", None),
            P(None, "feat"),
        ),
        check_vma=False,
    )
```
